32 devices in a mesh: tensor: 4 (over x, core), context: 4 (over z), dp: 2 (over y).
Axes of the slice: x: 2, y: 2, z: 4, core: 2. Of those that a mesh axis runs over, the one named last changes fastest.
Arguments:
- queries: bfloat16 [2, 512, 4096], P('dp', 'context', 'tensor'), may hold values from -6 to 6
- key_gates: bfloat16 [2, 512, 4096], P('dp', 'context', 'tensor'), may hold values from -6 to 6
- values: bfloat16 [2, 512, 4096], P('dp', 'context', 'tensor'), may hold values from -6 to 6
- out_grad: bfloat16 [2, 512, 4096], P('dp', 'context', 'tensor'), may hold values from -6 to 6
- featurizer: bfloat16 [3, 3, 4096], P(None, None, 'tensor'), may hold values from -3.5 to 3.5
- long_filter: bfloat16 [512, 4096], P('context', 'tensor'), may hold values from -2 to 2
Outputs:
- output: bfloat16 [2, 512, 4096], P('dp', 'context', 'tensor')
- grad_queries: bfloat16 [2, 512, 4096], P('dp', 'context', 'tensor')
- grad_keys: bfloat16 [2, 512, 4096], P('dp', 'context', 'tensor')
- grad_values: bfloat16 [2, 512, 4096], P('dp', 'context', 'tensor')
- grad_long: bfloat16 [512, 4096], P('context', 'tensor')
The draws below stay inside these ranges and needn't reach their ends.
All inputs are finite; a program needn't handle non-finite values.
Results may differ from the reference program's by a relative error of at most 0.015.
Values may be sent and summed in bfloat16 or wider, within the bound.
No kernel may reach another device: no remote copies, remote signals or barrier semaphores. Data moves between devices by JAX's collectives and lax.ppermute only.
A program may use at most 64 MiB of HBM per device.

```python
import jax
import jax.numpy as jnp
from jax import lax

D = 4096
KTAPS = 3
SEQ_LEN = 512
SEQS = 2


def draw_long_filter(key, part):
    subkeys = jax.random.split(key, 10)
    delay_offsets = jnp.arange(SEQ_LEN, dtype=jnp.float32)[:, None]
    chooser = jax.random.uniform(subkeys[0], (1, D))
    fast_len = jax.random.uniform(subkeys[1], (1, D), minval=30.0, maxval=50.0)
    slow_len = SEQ_LEN * jax.random.uniform(subkeys[2], (1, D), minval=1.0, maxval=8.0)
    fast_share = 0.5
    is_fast = chooser < fast_share
    decay_len = jnp.where(is_fast, fast_len, slow_len)
    decay_window = jnp.exp(-delay_offsets / decay_len)
    token_places = jax.random.randint(subkeys[3], (3, D), 1, SEQ_LEN)
    dropped_entries = jax.random.uniform(subkeys[4], (3, D), minval=0.5, maxval=0.8)
    for impulse_spike in range(3):
        decay_window = decay_window * jnp.where(delay_offsets >= token_places[impulse_spike][None, :].astype(jnp.float32), dropped_entries[impulse_spike][None, :], 1.0)
    amplitude = 1.5 / jnp.sqrt(jnp.minimum(decay_len, float(SEQ_LEN)))
    noise = jnp.clip(jax.random.normal(subkeys[5], (SEQ_LEN, D)), -4.0, 4.0)
    value = noise * decay_window * amplitude
    echo_start = jax.random.randint(subkeys[7], (1, D), SEQ_LEN // 8, SEQ_LEN // 2).astype(jnp.float32)
    echo_len = float(SEQ_LEN) * jax.random.uniform(subkeys[8], (1, D), minval=0.5, maxval=2.0)
    echo_noise = jnp.clip(jax.random.normal(subkeys[9], (SEQ_LEN, D)), -4.0, 4.0)
    echo_window = jnp.where(delay_offsets >= echo_start, jnp.exp(-jnp.maximum(delay_offsets - echo_start, 0.0) / echo_len), 0.0)
    echo_term = echo_noise * echo_window * (2.0 / jnp.sqrt(float(SEQ_LEN)))
    value = value + jnp.where(is_fast, echo_term, 0.0)
    direct = jax.random.uniform(subkeys[6], (1, D), minval=-2.0, maxval=2.0)
    value = jnp.where(delay_offsets == 0.0, direct, value)
    return jnp.clip(value, -2.0, 2.0).astype(jnp.bfloat16)


def block_levels(own_key, dims, cuts, low, largest):
    level = 1.0
    for axis_at, shards_of in cuts:
        heights = jax.random.uniform(jax.random.fold_in(jax.random.fold_in(own_key, 6), axis_at), (shards_of,), jnp.float32, low / len(cuts), largest / len(cuts))
        level = level * jnp.repeat(jnp.exp(heights), dims[axis_at] // shards_of).reshape((-1,) + (1,) * (len(dims) - 1 - axis_at))
    return level


def centred(own_key, extent, spread, limit, pieces=(), kind=jnp.bfloat16):
    drawn = jax.random.normal(own_key, extent, jnp.float32) * spread
    if len(pieces) > 0:
        drawn = block_levels(own_key, extent, pieces, -0.22, 0.18) * drawn
    return jnp.clip(drawn, min=-limit, max=limit).astype(kind)


def setup_inputs(seed: int = 0) -> dict:
    splits = jax.random.split(jax.random.key(seed), 7)
    return {
        "queries": centred(splits[0], (SEQS, SEQ_LEN, D), 1.0, 6.0, ((0, 2), (1, 4), (2, 4))),
        "key_gates": centred(splits[1], (SEQS, SEQ_LEN, D), 1.0, 6.0, ((0, 2), (1, 4), (2, 4))),
        "values": centred(splits[2], (SEQS, SEQ_LEN, D), 1.0, 6.0, ((0, 2), (1, 4), (2, 4))),
        "out_grad": centred(splits[3], (SEQS, SEQ_LEN, D), 1.0, 6.0, ((0, 2), (1, 4), (2, 4))),
        "featurizer": centred(splits[4], (3, KTAPS, D), KTAPS ** -0.5, 3.5, ((2, 4),)),
        "long_filter": draw_long_filter(jax.random.fold_in(splits[6], 71), 0),
    }


def apply_taps(extended, tap_rows, along_axis, length, forward):
    tap_count = tap_rows.shape[0]
    tap_total = None
    for lag in range(tap_count):
        slice_start = tap_count - 1 - lag if forward else lag
        tap_piece = lax.slice_in_dim(extended, slice_start, slice_start + length, axis=along_axis)
        tap_term = tap_rows[lag] * tap_piece
        tap_total = tap_term if tap_total is None else tap_total + tap_term
    return tap_total


def causal_feat(signal, tap_rows):
    padded = jnp.pad(signal, ((0, 0), (tap_rows.shape[0] - 1, 0), (0, 0)))
    return apply_taps(padded, tap_rows, 1, signal.shape[1], True)


def anticausal_feat(signal, tap_rows):
    padded = jnp.pad(signal, ((0, 0), (0, tap_rows.shape[0] - 1), (0, 0)))
    return apply_taps(padded, tap_rows, 1, signal.shape[1], False)


def reference(queries, key_gates, values, out_grad, featurizer, long_filter):
    block_width = 256
    block_count = D // block_width
    length = SEQ_LEN
    spectrum_len = 2 * length

    def one_block(block_index):
        offset = block_index * block_width

        def slice_block(array):
            return lax.dynamic_slice_in_dim(array, offset, block_width, array.ndim - 1)

        query_block = slice_block(queries).astype(jnp.float32)
        key_block = slice_block(key_gates).astype(jnp.float32)
        value_block = slice_block(values).astype(jnp.float32)
        grad_block = slice_block(out_grad).astype(jnp.float32)
        feat_block = slice_block(featurizer).astype(jnp.float32)
        query_feat = causal_feat(query_block, feat_block[0]).astype(jnp.bfloat16).astype(jnp.float32)
        key_feat = causal_feat(key_block, feat_block[1]).astype(jnp.bfloat16).astype(jnp.float32)
        value_features = causal_feat(value_block, feat_block[2]).astype(jnp.bfloat16).astype(jnp.float32)
        gated = (key_feat * value_features).astype(jnp.bfloat16)
        signal_grad = (grad_block * query_feat).astype(jnp.bfloat16)
        gated_spec = jnp.fft.rfft(gated.astype(jnp.float32), n=spectrum_len, axis=1)
        filter_spec = jnp.fft.rfft(slice_block(long_filter).astype(jnp.float32), n=spectrum_len, axis=0)[None]
        grad_spec = jnp.fft.rfft(signal_grad.astype(jnp.float32), n=spectrum_len, axis=1)
        conv_out = jnp.fft.irfft(gated_spec * filter_spec, n=spectrum_len, axis=1)[:, :length].astype(jnp.bfloat16)
        back_out = jnp.fft.irfft(grad_spec * jnp.conj(filter_spec), n=spectrum_len, axis=1)[:, :length].astype(jnp.bfloat16)
        filter_terms = jnp.fft.irfft(grad_spec * jnp.conj(gated_spec), n=spectrum_len, axis=1)[:, :length]
        filter_grad = jnp.sum(filter_terms, axis=0).astype(jnp.bfloat16)
        conv_wide = conv_out.astype(jnp.float32)
        back_wide = back_out.astype(jnp.float32)
        output = (query_feat * conv_wide).astype(jnp.bfloat16)
        query_feat_grad = (grad_block * conv_wide).astype(jnp.bfloat16).astype(jnp.float32)
        key_feat_grad = (back_wide * value_features).astype(jnp.bfloat16).astype(jnp.float32)
        value_feat_grad = (back_wide * key_feat).astype(jnp.bfloat16).astype(jnp.float32)
        grad_queries = anticausal_feat(query_feat_grad, feat_block[0]).astype(jnp.bfloat16)
        grad_keys = anticausal_feat(key_feat_grad, feat_block[1]).astype(jnp.bfloat16)
        grad_values = anticausal_feat(value_feat_grad, feat_block[2]).astype(jnp.bfloat16)
        return output, grad_queries, grad_keys, grad_values, filter_grad

    blocks = lax.map(one_block, jnp.arange(block_count, dtype=jnp.int32))

    def assemble(stacked):
        return jnp.moveaxis(stacked, 0, 2).reshape(stacked.shape[1], stacked.shape[2], block_count * block_width)

    grad_long = jnp.moveaxis(blocks[4], 0, 1).reshape(length, block_count * block_width)
    return assemble(blocks[0]), assemble(blocks[1]), assemble(blocks[2]), assemble(blocks[3]), grad_long
```

```python
import functools
import math

import jax
import jax.numpy as jnp
import numpy as np
from jax import lax
from jax.experimental import pallas as pl
from jax.experimental.pallas import tpu as pltpu
from jax.sharding import PartitionSpec as P


def from_behind(block, axis, distance):
    devices = range(lax.axis_size(axis))
    route = [(i - distance, i) for i in devices if i - distance in devices]
    return lax.ppermute(block, axis, route)


def apply_taps(extended, tap_rows, along_axis, length, forward):
    tap_count = tap_rows.shape[0]
    tap_total = None
    for lag in range(tap_count):
        slice_start = tap_count - 1 - lag if forward else lag
        tap_piece = lax.slice_in_dim(extended, slice_start, slice_start + length, axis=along_axis)
        tap_term = tap_rows[lag] * tap_piece
        tap_total = tap_term if tap_total is None else tap_total + tap_term
    return tap_total


def dft_table(length, rows, columns, direction):
    first = jnp.arange(rows, dtype=jnp.int32)
    second = jnp.arange(columns, dtype=jnp.int32)
    product = first[:, None] * second[None, :] % length
    angle = 2.0 * math.pi / length * product.astype(jnp.float32)
    return (jnp.cos(angle), direction * jnp.sin(angle))


def factor_sizes(length):
    chosen = 1
    for option in range(1, math.isqrt(2 * length) + 1):
        if length % option == 0:
            chosen = option
    return (chosen, 2 * length // chosen)


def contract(form, left, right):
    return jnp.einsum(form, left, right, precision=lax.Precision.HIGHEST)


def forward_spectrum(signal):
    rows, length = signal.shape
    inner, outer = factor_sizes(length)
    half = outer // 2
    grid = signal.reshape(rows, half, inner)
    first_cos, first_sin = dft_table(outer, half, outer, -1.0)
    section_real = contract("rqp,qk->rkp", grid, first_cos)
    section_imag = contract("rqp,qk->rkp", grid, first_sin)
    twist_cos, twist_sin = dft_table(2 * length, outer, inner, -1.0)
    turned_real = section_real * twist_cos - section_imag * twist_sin
    turned_imag = section_real * twist_sin + section_imag * twist_cos
    second_cos, second_sin = dft_table(inner, inner, inner, -1.0)
    final_real = contract("rkp,pj->rkj", turned_real, second_cos) - contract(
        "rkp,pj->rkj", turned_imag, second_sin
    )
    final_imag = contract("rkp,pj->rkj", turned_real, second_sin) + contract(
        "rkp,pj->rkj", turned_imag, second_cos
    )
    return (final_real, final_imag)


def inverse_spectrum(spec_real, spec_imag, length):
    rows = spec_real.shape[0]
    inner, outer = factor_sizes(length)
    half = outer // 2
    second_cos, second_sin = dft_table(inner, inner, inner, 1.0)
    section_real = contract("rkj,jp->rkp", spec_real, second_cos) - contract(
        "rkj,jp->rkp", spec_imag, second_sin
    )
    section_imag = contract("rkj,jp->rkp", spec_real, second_sin) + contract(
        "rkj,jp->rkp", spec_imag, second_cos
    )
    twist_cos, twist_sin = dft_table(2 * length, outer, inner, 1.0)
    turned_real = section_real * twist_cos - section_imag * twist_sin
    turned_imag = section_real * twist_sin + section_imag * twist_cos
    first_cos, first_sin = dft_table(outer, outer, half, 1.0)
    final_real = contract("rkp,kq->rqp", turned_real, first_cos) - contract(
        "rkp,kq->rqp", turned_imag, first_sin
    )
    final_imag = contract("rkp,kq->rqp", turned_real, first_sin) + contract(
        "rkp,kq->rqp", turned_imag, first_cos
    )
    return (final_real.reshape(rows, length), final_imag.reshape(rows, length))


def long_terms(signal, filt_rows, signal_grad):
    rows, length = signal.shape
    scale = 1.0 / (2 * length)
    stacked = jnp.concatenate([signal, filt_rows, signal_grad], axis=0).astype(jnp.float32)
    spec_real, spec_imag = forward_spectrum(stacked)
    sig_real, filt_real, grad_real = (
        spec_real[:rows],
        spec_real[rows : 2 * rows],
        spec_real[2 * rows :],
    )
    sig_imag, filt_imag, grad_imag = (
        spec_imag[:rows],
        spec_imag[rows : 2 * rows],
        spec_imag[2 * rows :],
    )
    ahead_real = sig_real * filt_real - sig_imag * filt_imag
    ahead_imag = sig_real * filt_imag + sig_imag * filt_real
    behind_real = grad_real * filt_real + grad_imag * filt_imag
    behind_imag = grad_imag * filt_real - grad_real * filt_imag
    cross_real = grad_real * sig_real + grad_imag * sig_imag
    cross_imag = grad_imag * sig_real - grad_real * sig_imag
    joined_real = jnp.concatenate([ahead_real - behind_imag, cross_real], axis=0)
    joined_imag = jnp.concatenate([ahead_imag + behind_real, cross_imag], axis=0)
    back_real, back_imag = inverse_spectrum(joined_real, joined_imag, length)
    return (back_real[:rows] * scale, back_imag[:rows] * scale, back_real[rows:] * scale)


TILE = 16
LANES = 128
TABLE_LIMIT = 1 << 20


def transform_tables(length):
    angle = np.outer(2 * np.arange(length) + 1, np.arange(length)) % (4 * length)
    angle = np.pi / (2.0 * length) * angle
    ahead = np.concatenate([np.cos(angle), np.sin(angle)], axis=0)
    high = ahead.astype(jnp.bfloat16)
    low = (ahead - high.astype(np.float64)).astype(jnp.bfloat16)
    behind = (ahead.T / length).astype(jnp.bfloat16)
    return high, low, behind


def row_index(shape):
    return lax.broadcasted_iota(jnp.int32, shape, 0)


def earlier(rows, lag, rim):
    if lag == 0:
        return rows
    moved = pltpu.roll(rows, lag, 0)
    index = row_index(rows.shape)
    for at in range(lag):
        moved = jnp.where(index == at, rim[len(rim) - lag + at], moved)
    return moved


def later(rows, lag, rim):
    if lag == 0:
        return rows
    count = rows.shape[0]
    moved = pltpu.roll(rows, count - lag, 0)
    index = row_index(rows.shape)
    for at in range(lag):
        moved = jnp.where(index == count - lag + at, rim[at], moved)
    return moved


def rounded(value):
    return value.astype(jnp.bfloat16).astype(jnp.float32)


def weighted(terms, tap_rows):
    total = None
    for term, tap in zip(terms, tap_rows):
        part = tap * term
        total = part if total is None else total + part
    return total


def tap_list(taps_ref, which, columns=slice(None)):
    count = taps_ref.shape[0] // 3
    return [taps_ref[which * count + lag : which * count + lag + 1, columns] for lag in range(count)]


def one_row(rows, at):
    return rows[at : at + 1, :]


def before_kernel(peers_dp, q_ref, k_ref, v_ref, g_ref, taps_ref, filt_ref, out_ref):
    tokens, width = q_ref.shape
    rim = taps_ref.shape[0] // 3 - 1
    share = filt_ref.shape[0] // peers_dp
    blank = [jnp.zeros((1, width), jnp.float32)] * rim
    wide = [ref[...].astype(jnp.float32) for ref in (q_ref, k_ref, v_ref, g_ref)]
    feats = []
    for which in range(3):
        terms = [earlier(wide[which], lag, blank) for lag in range(rim + 1)]
        feats.append(rounded(weighted(terms, tap_list(taps_ref, which))))
    gated = (feats[1] * feats[2]).astype(jnp.bfloat16)
    grad = (wide[3] * feats[0]).astype(jnp.bfloat16)
    start = pl.multiple_of(lax.axis_index("dp") * share, TILE)
    filt = filt_ref[pl.ds(start, share), :]
    edge = jnp.zeros((TILE, width), jnp.float32)
    index = row_index(edge.shape)
    at = 0
    for which, first in [(w, True) for w in range(4)] + [(w, False) for w in range(3)]:
        for step in range(rim):
            row = one_row(wide[which], step if first else tokens - rim + step)
            edge = jnp.where(index == at, row, edge)
            at += 1
    edge = edge.astype(jnp.bfloat16)
    for block in range(width // LANES):
        lanes = slice(block * LANES, (block + 1) * LANES)
        out_ref[block, :tokens, :] = gated[:, lanes]
        out_ref[block, tokens : 2 * tokens, :] = grad[:, lanes]
        out_ref[block, 2 * tokens : 2 * tokens + share, :] = filt[:, lanes]
        out_ref[block, 2 * tokens + share :, :] = edge[:, lanes]


def middle_kernel(context, dp, tokens, in_ref, taps_ref, high_ref, low_ref, behind_ref, out_ref, mat_ref, spec_ref):
    length = context * tokens
    share = tokens // dp
    rim = taps_ref.shape[0] // 3 - 1
    taps = [tap_list(taps_ref, which) for which in range(3)]
    zero = jnp.zeros((1, LANES), jnp.float32)

    edges = {}
    for at in range(context):
        for seq in range(dp):
            edges[at, seq] = in_ref[at * dp + seq, 2 * tokens + share :, :].astype(jnp.float32)

    def head(at, seq, which):
        if at >= context:
            return [zero] * rim
        return [one_row(edges[at, seq], which * rim + step) for step in range(rim)]

    def tail(at, seq, which):
        if at < 0:
            return [zero] * rim
        return [one_row(edges[at, seq], (4 + which) * rim + step) for step in range(rim)]

    for at in range(context):
        span = slice(at * tokens, (at + 1) * tokens)
        for seq in range(dp):
            source = at * dp + seq
            feats = []
            for which in range(3):
                line = tail(at - 1, seq, which) + head(at, seq, which)
                feats.append(
                    [
                        rounded(weighted([line[rim + step - lag] for lag in range(rim + 1)], taps[which]))
                        for step in range(rim)
                    ]
                )
            grads = head(at, seq, 3)
            first = in_ref[source, :TILE, :].astype(jnp.float32)
            second = in_ref[source, tokens : tokens + TILE, :].astype(jnp.float32)
            index = row_index(first.shape)
            for step in range(rim):
                first = jnp.where(index == step, feats[1][step] * feats[2][step], first)
                second = jnp.where(index == step, grads[step] * feats[0][step], second)
            lanes = slice(seq * LANES, (seq + 1) * LANES)
            far_lanes = slice((dp + seq) * LANES, (dp + seq + 1) * LANES)
            mat_ref[at * tokens : at * tokens + TILE, lanes] = first.astype(jnp.bfloat16)
            mat_ref[at * tokens + TILE : (at + 1) * tokens, lanes] = in_ref[source, TILE:tokens, :]
            mat_ref[at * tokens : at * tokens + TILE, far_lanes] = second.astype(jnp.bfloat16)
            mat_ref[at * tokens + TILE : (at + 1) * tokens, far_lanes] = in_ref[source, tokens + TILE : 2 * tokens, :]
            begin = at * tokens + seq * share
            mat_ref[begin : begin + share, 2 * dp * LANES :] = in_ref[source, 2 * tokens : 2 * tokens + share, :]

    chunk = min(length, 128)

    def dot(left, right):
        return jnp.dot(left, right, preferred_element_type=jnp.float32)

    for begin in range(0, length, chunk):
        near = slice(begin, begin + chunk)
        far = slice(length + begin, length + begin + chunk)
        mat = mat_ref[...]
        real = dot(high_ref[near, :], mat) + dot(low_ref[near, :], mat)
        imag = dot(high_ref[far, :], mat) + dot(low_ref[far, :], mat)

        def part(which):
            lanes = slice(which * LANES, (which + 1) * LANES)
            return real[:, lanes], imag[:, lanes]

        filt_r, filt_i = part(2 * dp)
        cross_r = cross_i = None
        for seq in range(dp):
            sig_r, sig_i = part(seq)
            grad_r, grad_i = part(dp + seq)
            lanes = slice(seq * LANES, (seq + 1) * LANES)
            far_lanes = slice((dp + seq) * LANES, (dp + seq + 1) * LANES)
            spec_ref[near, lanes] = (sig_r * filt_r - sig_i * filt_i).astype(jnp.bfloat16)
            spec_ref[far, lanes] = (sig_r * filt_i + sig_i * filt_r).astype(jnp.bfloat16)
            spec_ref[near, far_lanes] = (grad_r * filt_r + grad_i * filt_i).astype(jnp.bfloat16)
            spec_ref[far, far_lanes] = (grad_i * filt_r - grad_r * filt_i).astype(jnp.bfloat16)
            term_r = grad_r * sig_r + grad_i * sig_i
            term_i = grad_i * sig_r - grad_r * sig_i
            cross_r = term_r if cross_r is None else cross_r + term_r
            cross_i = term_i if cross_i is None else cross_i + term_i
        spec_ref[near, 2 * dp * LANES :] = cross_r.astype(jnp.bfloat16)
        spec_ref[far, 2 * dp * LANES :] = cross_i.astype(jnp.bfloat16)

    blank = [zero] * rim
    after = {}
    for at in reversed(range(context)):
        span = slice(at * tokens, (at + 1) * tokens)
        waves = dot(behind_ref[span, :], spec_ref[...])
        cross = waves[:, 2 * dp * LANES :].astype(jnp.bfloat16)
        for seq in range(dp):
            target = at * dp + seq
            conv = waves[:, seq * LANES : (seq + 1) * LANES]
            back = waves[:, (dp + seq) * LANES : (dp + seq + 1) * LANES]
            out_ref[target, :tokens, :] = conv.astype(jnp.bfloat16)
            out_ref[target, tokens : 2 * tokens, :] = back.astype(jnp.bfloat16)
            out_ref[target, 2 * tokens : 3 * tokens, :] = cross
            lines = []
            for which in range(3):
                lines += tail(at - 1, seq, which)
            for which in (1, 2, 3):
                lines += head(at + 1, seq, which)
            for rows in after.get(seq, (blank, blank)):
                lines += rows
            edge = jnp.zeros((TILE, LANES), jnp.float32)
            index = row_index(edge.shape)
            for place, line in enumerate(lines):
                edge = jnp.where(index == place, line, edge)
            out_ref[target, 3 * tokens :, :] = edge.astype(jnp.bfloat16)
            after[seq] = (
                [one_row(conv, step) for step in range(rim)],
                [one_row(back, step) for step in range(rim)],
            )


def after_kernel(in_ref, q_ref, k_ref, v_ref, g_ref, taps_ref, out_ref, gq_ref, gk_ref, gv_ref, gl_ref):
    tokens, width = q_ref.shape
    rim = taps_ref.shape[0] // 3 - 1
    for block in range(width // LANES):
        lanes = slice(block * LANES, (block + 1) * LANES)
        conv = in_ref[block, :tokens, :].astype(jnp.float32)
        back = in_ref[block, tokens : 2 * tokens, :].astype(jnp.float32)
        gl_ref[:, lanes] = in_ref[block, 2 * tokens : 3 * tokens, :]
        edge = in_ref[block, 3 * tokens :, :].astype(jnp.float32)

        def lines(place):
            return [one_row(edge, place * rim + step) for step in range(rim)]

        taps = [tap_list(taps_ref, which, lanes) for which in range(3)]
        wide = [ref[:, lanes].astype(jnp.float32) for ref in (q_ref, k_ref, v_ref, g_ref)]
        feats = []
        for which in range(3):
            terms = [earlier(wide[which], lag, lines(which)) for lag in range(rim + 1)]
            feats.append(rounded(weighted(terms, taps[which])))
        past = []
        for which in (1, 2):
            line = [one_row(wide[which], tokens - rim + step) for step in range(rim)] + lines(2 + which)
            past.append(
                [
                    rounded(weighted([line[rim + step - lag] for lag in range(rim + 1)], taps[which]))
                    for step in range(rim)
                ]
            )
        past_grad, past_conv, past_back = lines(5), lines(6), lines(7)
        out_ref[:, lanes] = (feats[0] * conv).astype(jnp.bfloat16)
        flows = (
            (rounded(wide[3] * conv), [rounded(past_grad[s] * past_conv[s]) for s in range(rim)]),
            (rounded(back * feats[2]), [rounded(past_back[s] * past[1][s]) for s in range(rim)]),
            (rounded(back * feats[1]), [rounded(past_back[s] * past[0][s]) for s in range(rim)]),
        )
        for which, ref in enumerate((gq_ref, gk_ref, gv_ref)):
            rows, rest = flows[which]
            terms = [later(rows, lag, rest) for lag in range(rim + 1)]
            ref[:, lanes] = weighted(terms, taps[which]).astype(jnp.bfloat16)


def on_device(queries, key_gates, values, out_grad, featurizer, long_filter):
    context, dp = lax.axis_size("context"), lax.axis_size("dp")
    peers = context * dp
    _, tokens, channels = queries.shape
    length = context * tokens
    rim = featurizer.shape[1] - 1
    fits = (
        channels == peers * LANES
        and long_filter.shape[0] == tokens
        and tokens % (dp * TILE) == 0
        and 8 * rim <= TILE
        and 2 * length * length <= TABLE_LIMIT
    )
    if not fits:
        return factored(queries, key_gates, values, out_grad, featurizer, long_filter)

    rows = (queries[0], key_gates[0], values[0], out_grad[0])
    taps = featurizer.astype(jnp.float32).reshape(-1, channels)
    share = tokens // dp
    sent = 2 * tokens + share + TILE
    steps = 4
    width = channels // steps
    column = lambda count: pl.BlockSpec((count, width), lambda i: (0, i))
    stacked = lambda count: pl.BlockSpec((width // LANES, count, LANES), lambda i: (i, 0, 0))
    send = pl.pallas_call(
        functools.partial(before_kernel, dp),
        out_shape=jax.ShapeDtypeStruct((peers, sent, LANES), jnp.bfloat16),
        grid=(steps,),
        in_specs=[column(tokens)] * 4 + [column(taps.shape[0]), column(tokens)],
        out_specs=stacked(sent),
        name="before",
    )(*rows, taps, long_filter)
    came = lax.all_to_all(send, ("context", "dp"), split_axis=0, concat_axis=0, tiled=True)
    place = lax.axis_index("context") * dp + lax.axis_index("dp")
    own_taps = lax.dynamic_slice_in_dim(taps, place * LANES, LANES, axis=1)
    high, low, behind = transform_tables(length)
    back = pl.pallas_call(
        functools.partial(middle_kernel, context, dp, tokens),
        out_shape=jax.ShapeDtypeStruct((peers, 3 * tokens + TILE, LANES), jnp.bfloat16),
        scratch_shapes=[
            pltpu.VMEM((length, (2 * dp + 1) * LANES), jnp.bfloat16),
            pltpu.VMEM((2 * length, (2 * dp + 1) * LANES), jnp.bfloat16),
        ],
        name="middle",
    )(came, own_taps, jnp.asarray(high), jnp.asarray(low), jnp.asarray(behind))
    home = lax.all_to_all(back, ("context", "dp"), split_axis=0, concat_axis=0, tiled=True)
    whole = jax.ShapeDtypeStruct((tokens, channels), jnp.bfloat16)
    output, grad_queries, grad_keys, grad_values, grad_long = pl.pallas_call(
        after_kernel,
        out_shape=[whole] * 5,
        grid=(steps,),
        in_specs=[stacked(3 * tokens + TILE)] + [column(tokens)] * 4 + [column(taps.shape[0])],
        out_specs=[column(tokens)] * 5,
        name="after",
    )(home, *rows, taps)
    return (output[None], grad_queries[None], grad_keys[None], grad_values[None], grad_long)


def factored(queries, key_gates, values, out_grad, featurizer, long_filter):
    query_rows = queries[0]
    key_rows = key_gates[0]
    value_rows = values[0]
    grad_rows = out_grad[0]
    tap_count = featurizer.shape[1]
    tokens = query_rows.shape[0]
    feat_wide = featurizer.astype(jnp.float32)
    rim_query, rim_key, rim_value = from_behind(
        (
            query_rows[tokens - (tap_count - 1) :],
            key_rows[tokens - (tap_count - 1) :],
            value_rows[tokens - (tap_count - 1) :],
        ),
        "context",
        1,
    )

    def featured(rim_rows, rows, which):
        extended = jnp.concatenate([rim_rows, rows], axis=0).astype(jnp.float32)
        return (
            apply_taps(extended, feat_wide[which], 0, tokens, True)
            .astype(jnp.bfloat16)
            .astype(jnp.float32)
        )

    query_feat = featured(rim_query, query_rows, 0)
    key_feat = featured(rim_key, key_rows, 1)
    value_features = featured(rim_value, value_rows, 2)
    grad_wide = grad_rows.astype(jnp.float32)
    gated = (key_feat * value_features).astype(jnp.bfloat16)
    signal_grad = (grad_wide * query_feat).astype(jnp.bfloat16)
    arrived = (
        lax.all_to_all(gated.T, "context", split_axis=0, concat_axis=1, tiled=True),
        lax.all_to_all(long_filter.T, "context", split_axis=0, concat_axis=1, tiled=True),
        lax.all_to_all(signal_grad.T, "context", split_axis=0, concat_axis=1, tiled=True),
    )
    conv_part, back_part, filter_part = long_terms(arrived[0], arrived[1], arrived[2])
    conv_cols, back_cols = (
        lax.all_to_all(
            conv_part.astype(jnp.bfloat16), "context", split_axis=1, concat_axis=0, tiled=True
        ),
        lax.all_to_all(
            back_part.astype(jnp.bfloat16), "context", split_axis=1, concat_axis=0, tiled=True
        ),
    )
    conv_wide = conv_cols.T.astype(jnp.float32)
    back_wide = back_cols.T.astype(jnp.float32)
    output = (query_feat * conv_wide).astype(jnp.bfloat16)[None]
    query_feat_grad = (grad_wide * conv_wide).astype(jnp.bfloat16)
    key_feat_grad = (back_wide * value_features).astype(jnp.bfloat16)
    value_feat_grad = (back_wide * key_feat).astype(jnp.bfloat16)
    after_query, after_key, after_value = from_behind(
        (
            query_feat_grad[: tap_count - 1],
            key_feat_grad[: tap_count - 1],
            value_feat_grad[: tap_count - 1],
        ),
        "context",
        -1,
    )

    def unfeatured(rows, after_rows, which):
        extended = jnp.concatenate([rows, after_rows], axis=0).astype(jnp.float32)
        return apply_taps(extended, feat_wide[which], 0, tokens, False).astype(jnp.bfloat16)[None]

    grad_queries = unfeatured(query_feat_grad, after_query, 0)
    grad_keys = unfeatured(key_feat_grad, after_key, 1)
    grad_values = unfeatured(value_feat_grad, after_value, 2)
    filter_sum = lax.psum(filter_part, "dp").astype(jnp.bfloat16)
    filter_cols = lax.all_to_all(filter_sum, "context", split_axis=1, concat_axis=0, tiled=True)
    grad_long = filter_cols.T
    return (output, grad_queries, grad_keys, grad_values, grad_long)


def solution(mesh):
    in_specs = (
        P("dp", "context", "tensor"),
        P("dp", "context", "tensor"),
        P("dp", "context", "tensor"),
        P("dp", "context", "tensor"),
        P(None, None, "tensor"),
        P("context", "tensor"),
    )
    out_specs = (
        P("dp", "context", "tensor"),
        P("dp", "context", "tensor"),
        P("dp", "context", "tensor"),
        P("dp", "context", "tensor"),
        P("context", "tensor"),
    )
    return jax.shard_map(
        on_device, mesh=mesh, in_specs=in_specs, out_specs=out_specs, check_vma=False
    )
```
